32 devices in a mesh: ep: 8 (over y, x, core), sq: 4 (over z).
Axes of the slice: x: 2, y: 2, z: 4, core: 2. Of those that a mesh axis runs over, the one named last changes fastest.
Arguments:
- block_input: bfloat16 [16, 512, 768], P('ep', 'sq'), may hold values from -6 to 6
- cotangent: bfloat16 [16, 512, 768], P('ep', 'sq'), may hold values from -6 to 6
- routes: int32 [16, 512, 2], P('ep', 'sq'), may hold values from 0 to 15, all different within a row; in each aligned block of 128 rows (0 to 127, 128 to 255, ..., all dimensions but the last counted through in order) at most 24 rows name the same one
- buckets: int32 [512, 512], P('sq'), may hold values from 0 to 31
- position_bias: float32 [32, 12], replicated, may hold values from -2 to 242
- attn_gain: bfloat16 [768], P(('ep', 'sq')), may hold values from 0.5 to 1.5
- ffn_gain: bfloat16 [768], P(('ep', 'sq')), may hold values from 0.5 to 1.5
- qkv_weight: bfloat16 [768, 2304], P(('ep', 'sq')), may hold values from -0.21875 to 0.21875
- attn_out: bfloat16 [768, 768], P(('ep', 'sq')), may hold values from -0.875 to 0.875
- router_weight: bfloat16 [768, 16], P(('ep', 'sq')), may hold values from -0.21875 to 0.21875
- expert_in: bfloat16 [16, 768, 3072], P('ep', None, 'sq'), may hold values from -0.21875 to 0.21875
- expert_out: bfloat16 [16, 3072, 768], P('ep', 'sq'), may hold values from -0.15625 to 0.15625
Outputs:
- block_output: bfloat16 [16, 512, 768], P('ep', 'sq')
- input_grad: float32 [16, 512, 768], P('ep', 'sq')
- bias_grad: float32 [32, 12], replicated
- attn_gain_grad: float32 [768], P(('ep', 'sq'))
- ffn_gain_grad: float32 [768], P(('ep', 'sq'))
- qkv_grad: float32 [768, 2304], P(('ep', 'sq'))
- attn_out_grad: float32 [768, 768], P(('ep', 'sq'))
- router_grad: float32 [768, 16], P(('ep', 'sq'))
- expert_in_grad: float32 [16, 768, 3072], P('ep', None, 'sq')
- expert_out_grad: float32 [16, 3072, 768], P('ep', 'sq')
The draws below stay inside these ranges and needn't reach their ends.
Inputs may be any that keep to these rules, and one draw needn't show every extreme that they name: `routes`: each token names two different experts. Within each aligned block of positions that one device holds of one sequence, no expert is named more than max(2, 3 x block length / number of experts) times (24 here: 1.5 times the mean), a bound that some block reaches.
All inputs are finite; a program needn't handle non-finite values.
Results may differ from the reference program's by a relative error of at most 0.017.
Values may be sent and summed in bfloat16 or wider, within the bound.
A program may use at most 192 MiB of HBM per device.

```python
import math
import jax
import jax.numpy as jnp
import numpy as np
from jax import lax

D = 768
HEADS = 12
FF = 3072
EXPERTS = 16
BUCKETS = 32
SEQ_LEN = 512
NSEQ = 16
BLOCK_LEN = 128
MOST = 24


def draw_position_bias(key, part):
    base = jnp.clip(jax.random.normal(key, (BUCKETS, HEADS), jnp.float32) * 0.5, -2.0, 2.0)
    return base


def set_ends(drawn, rng, low, top_value):
    longest = drawn.shape.index(max(drawn.shape))
    spots = []
    for shift in (0, 1):
        where = [jax.random.randint(jax.random.fold_in(rng, axis), (), 0, length) for axis, length in enumerate(drawn.shape)]
        where[longest] = (where[longest] + shift) % drawn.shape[longest]
        spots.append(tuple(where))
    return drawn.at[spots[0]].set(low).at[spots[1]].set(top_value)


def block_levels(stream_key, extent, split, low, largest):
    factor_of = 1.0
    for dim, parts in split:
        draws = jax.random.uniform(jax.random.fold_in(jax.random.fold_in(stream_key, 6), dim), (parts,), jnp.float32, low / len(split), largest / len(split))
        factor_of = factor_of * jnp.repeat(jnp.exp(draws), extent[dim] // parts).reshape((-1,) + (1,) * (len(extent) - 1 - dim))
    return factor_of


def assign_block(stream_key, own, number, rows, amount, top, reach, slope):
    ranking = jax.random.permutation(stream_key, amount)
    crowded, usual = shares(amount, rows * top, reach, slope, True), shares(amount, rows * top, reach, slope, False)
    places = jnp.arange(amount)

    def named(tallies, rotation):
        used = int((tallies > 0).sum())
        fixed = max(1, used // 4)
        moved = fixed + (places - fixed + rotation * (used - fixed)) % max(1, amount - fixed)
        return jnp.zeros((amount,), jnp.int32).at[ranking[jnp.where(places < fixed, places, moved)]].set(jnp.asarray(tallies, jnp.int32))

    tallies = jnp.where(number % 4 == 0, named(crowded, number // 4), named(usual, number - number // 4 - 1))
    mixed = jax.random.permutation(jax.random.fold_in(own, 3), amount)
    giver, taker = mixed[0:amount // 2 * 2:2], mixed[1:amount // 2 * 2:2]
    margin = jnp.minimum(tallies[giver] - 1, reach - tallies[taker]) // 2
    margin = jnp.where((giver == ranking[0]) | (taker == ranking[0]) | (tallies[taker] == 0), 0, jnp.maximum(margin, 0))
    moved = jax.random.randint(jax.random.fold_in(own, 4), (amount // 2,), 0, 1 << 20) % (margin + 1)
    tallies = tallies.at[giver].add(-moved).at[taker].add(moved)
    items = jnp.searchsorted(jnp.cumsum(tallies), jnp.arange(rows * top), side="right").astype(jnp.int32)
    table = items.reshape(top, rows).T
    table = table[jax.random.permutation(jax.random.fold_in(own, 1), rows)]
    rotation = jax.random.randint(jax.random.fold_in(own, 2), (rows, 1), 0, top)
    return jnp.take_along_axis(table, (jnp.arange(top)[None, :] + rotation) % top, axis=1)


def shares(amount, total, reach, slope, full):
    portions = [(1 << 20) // math.isqrt(grade ** slope) + 1 for grade in range(1, amount + 1)]
    largest = reach if full else min(reach, max(-(-total // amount), total * portions[0] // sum(portions)))
    least = 1 if total - largest >= amount - 1 else 0
    given, spare = [largest] + [least] * (amount - 1), total - largest - least * (amount - 1)
    while spare > 0:
        movable = [i for i in range(1, amount) if given[i] < largest] or [i for i in range(1, amount) if given[i] < reach]
        whole, remaining = sum([portions[i] for i in movable]), spare
        for i in movable:
            more = min(reach - given[i], max(1, remaining * portions[i] // whole), spare)
            given[i] = given[i] + more
            spare = spare - more
    return np.array(given)


def gaussian(rng, shape, deviation, reach, split=(), kind=jnp.bfloat16):
    factor_of = block_levels(rng, shape, split, -0.22, 0.18) if split else 1.0
    drawn = jax.random.normal(rng, shape, jnp.float32) * deviation * factor_of
    return jnp.minimum(jnp.maximum(drawn, -reach), reach).astype(kind)


def setup_inputs(seed: int = 0) -> dict:
    keys = jax.random.split(jax.random.key(seed), 13)
    block_input = gaussian(keys[0], (NSEQ, SEQ_LEN, D), 1.0, 6.0, ((0, 8), (1, 4)))
    cotangent = gaussian(keys[1], (NSEQ, SEQ_LEN, D), 1.0, 6.0, ((0, 8), (1, 4)))
    routes_keys = jax.random.split(jax.random.fold_in(keys[2], 1), NSEQ * SEQ_LEN // BLOCK_LEN)
    routes_turns = jax.random.permutation(jax.random.fold_in(keys[2], 3), NSEQ * SEQ_LEN // BLOCK_LEN)
    routes = jax.vmap(lambda own, number: assign_block(jax.random.fold_in(keys[2], 2), own, number, BLOCK_LEN, EXPERTS, 2, MOST, 2))(routes_keys, routes_turns).reshape((NSEQ, SEQ_LEN, 2))
    buckets = set_ends(jax.random.randint(keys[3], (SEQ_LEN, SEQ_LEN), 0, BUCKETS), jax.random.fold_in(keys[3], 1), 0, BUCKETS - 1).astype(jnp.int32)
    position_bias = draw_position_bias(jax.random.fold_in(keys[12], 71), 0)
    attn_gain = jnp.clip(1.0 + 0.1 * jax.random.normal(keys[5], (D,), jnp.float32), 0.5, 1.5).astype(jnp.bfloat16)
    ffn_gain = jnp.clip(1.0 + 0.1 * jax.random.normal(keys[6], (D,), jnp.float32), 0.5, 1.5).astype(jnp.bfloat16)
    qkv_weight = gaussian(keys[7], (D, 3 * D), D ** -0.5, 0.21875, ((0, 32),))
    attn_out = gaussian(keys[8], (D, D), (D // 16) ** -0.5, 0.875, ((0, 32),))
    router_weight = gaussian(keys[9], (D, EXPERTS), D ** -0.5, 0.21875, ((0, 32),))
    expert_in = gaussian(keys[10], (EXPERTS, D, FF), D ** -0.5, 0.21875, ((0, 8), (2, 4)))
    expert_out = gaussian(keys[11], (EXPERTS, FF, D), (FF // 2) ** -0.5, 0.15625, ((0, 8), (1, 4)))
    return dict(block_input=block_input, cotangent=cotangent, routes=routes, buckets=buckets, position_bias=position_bias, attn_gain=attn_gain, ffn_gain=ffn_gain, qkv_weight=qkv_weight, attn_out=attn_out, router_weight=router_weight, expert_in=expert_in, expert_out=expert_out)


epsilon = 1e-06
masked_score = -1e+30

def rms_scale(values):
    return lax.rsqrt(lax.optimization_barrier(jnp.mean(values * values, axis=-1, keepdims=True)) + epsilon)

def norm_backward(values, inv_rms, gain_vec, upstream):
    weighted = upstream * gain_vec
    inner = lax.optimization_barrier(jnp.mean(weighted * values, axis=-1, keepdims=True))
    return inv_rms * (weighted - values * inv_rms * inv_rms * inner)

def gelu_grad(pre_gelu, upstream):
    unused_out, pullback = jax.vjp(jax.nn.gelu, pre_gelu)
    return pullback(upstream)[0]

def reference(block_input, cotangent, routes, buckets, position_bias, attn_gain, ffn_gain, qkv_weight, attn_out, router_weight, expert_in, expert_out):
    seq_total, seq_length, model_width = block_input.shape
    bucket_count, head_count = position_bias.shape
    head_size = model_width // head_count
    expert_count = expert_in.shape[0]
    score_scale = head_size ** (-0.5)
    bucket_hot = (buckets[:, :, None] == jnp.arange(bucket_count, dtype=jnp.int32)).astype(jnp.float32)
    bias_full = jnp.einsum('qkb,bh->hqk', bucket_hot, position_bias, precision=lax.Precision.HIGHEST)
    positions = jnp.arange(seq_length, dtype=jnp.int32)
    causal = positions[None, :] <= positions[:, None]

    def project_seq(seq_input):
        inputs_wide = seq_input.astype(jnp.float32)
        scale_one = rms_scale(inputs_wide)
        normed_one = (inputs_wide * scale_one * attn_gain).astype(jnp.bfloat16)
        project = jnp.dot(normed_one, qkv_weight, preferred_element_type=jnp.float32).astype(jnp.bfloat16)
        queries = project[:, :model_width].reshape(seq_length, head_count, head_size)
        key_rows = project[:, model_width:2 * model_width].reshape(seq_length, head_count, head_size)
        value_rows = project[:, 2 * model_width:].reshape(seq_length, head_count, head_size)
        raw = jnp.einsum('qhe,khe->hqk', queries.astype(jnp.float32), key_rows.astype(jnp.float32))
        scores = jnp.where(causal, raw * score_scale + bias_full, masked_score)
        return (inputs_wide, scale_one, normed_one, queries, key_rows, value_rows, scores)

    def attention_forward(seq_input):
        inputs_wide, scale_one, normed_one, queries, key_rows, value_rows, scores = project_seq(seq_input)
        row_top = lax.optimization_barrier(jnp.max(scores, axis=-1, keepdims=True))
        log_total = row_top + jnp.log(lax.optimization_barrier(jnp.sum(jnp.exp(scores - row_top), axis=-1, keepdims=True)))
        probs = jnp.exp(scores - log_total).astype(jnp.bfloat16)
        attended = jnp.einsum('hqk,khe->qhe', probs.astype(jnp.float32), value_rows.astype(jnp.float32))
        attended = attended.reshape(seq_length, model_width).astype(jnp.bfloat16)
        residual = inputs_wide + jnp.dot(attended, attn_out, preferred_element_type=jnp.float32)
        return (residual, attended, log_total)
    residual, attended_all, log_totals = lax.map(attention_forward, block_input)
    tokens = seq_total * seq_length
    residual_flat = residual.reshape(tokens, model_width)
    scale_two = rms_scale(residual_flat)
    normed_two = (residual_flat * scale_two * ffn_gain).astype(jnp.bfloat16)
    logits = jnp.dot(normed_two, router_weight, preferred_element_type=jnp.float32)
    route_flat = routes.reshape(tokens, 2)
    route_hot = (route_flat[:, :, None] == jnp.arange(expert_count, dtype=jnp.int32)).astype(jnp.float32)
    chosen = lax.optimization_barrier(jnp.sum(logits[:, None, :] * route_hot, axis=-1))
    first_gate = 1.0 / (1.0 + jnp.exp(chosen[:, 1] - chosen[:, 0]))
    gate_pair = jnp.stack([first_gate, 1.0 - first_gate], axis=1)
    blocks = tokens // BLOCK_LEN
    entry_expert = route_flat.reshape(blocks, 2 * BLOCK_LEN)
    entry_hot = (entry_expert[:, :, None] == jnp.arange(expert_count, dtype=jnp.int32)).astype(jnp.int32)
    earlier = jnp.cumsum(entry_hot, axis=1) - entry_hot
    slot_rank = lax.optimization_barrier(jnp.sum(earlier * entry_hot, axis=-1))
    slot_index = (jnp.arange(blocks, dtype=jnp.int32)[:, None] * MOST + slot_rank).reshape(tokens, 2).astype(jnp.int32)
    capacity = blocks * MOST
    spread_rows = jnp.broadcast_to(normed_two[:, None, :], (tokens, 2, model_width))
    dispatch_in = jnp.zeros((expert_count, capacity, model_width), jnp.bfloat16).at[route_flat, slot_index].set(spread_rows)

    def expert_forward(operands):
        slot_rows, weight_first, weight_second = operands
        pre_gelu = jnp.dot(slot_rows, weight_first, preferred_element_type=jnp.float32)
        activated = jax.nn.gelu(pre_gelu).astype(jnp.bfloat16)
        return jnp.dot(activated, weight_second, preferred_element_type=jnp.float32).astype(jnp.bfloat16)
    expert_result = lax.map(expert_forward, (dispatch_in, expert_in, expert_out))
    picked = expert_result[route_flat, slot_index].astype(jnp.float32)
    expert_mix = lax.optimization_barrier(jnp.sum(gate_pair[:, :, None] * picked, axis=1))
    block_output = (residual_flat + expert_mix).astype(jnp.bfloat16).reshape(seq_total, seq_length, model_width)
    upstream = cotangent.reshape(tokens, model_width).astype(jnp.float32)
    gate_grad = lax.optimization_barrier(jnp.sum(upstream[:, None, :] * picked, axis=-1))
    slot_grad = (gate_pair[:, :, None] * upstream[:, None, :]).astype(jnp.bfloat16)
    dispatch_grad = jnp.zeros((expert_count, capacity, model_width), jnp.bfloat16).at[route_flat, slot_index].set(slot_grad)

    def expert_backward(operands):
        slot_rows, slot_grads, weight_first, weight_second = operands
        pre_gelu = jnp.dot(slot_rows, weight_first, preferred_element_type=jnp.float32)
        activated = jax.nn.gelu(pre_gelu).astype(jnp.bfloat16)
        act_grad = jnp.dot(slot_grads, weight_second.T, preferred_element_type=jnp.float32)
        second_grad = jnp.dot(activated.T, slot_grads, preferred_element_type=jnp.float32)
        pre_grad = gelu_grad(pre_gelu, act_grad).astype(jnp.bfloat16)
        first_grad = jnp.dot(slot_rows.T, pre_grad, preferred_element_type=jnp.float32)
        slot_back = jnp.dot(pre_grad, weight_first.T, preferred_element_type=jnp.float32).astype(jnp.bfloat16)
        return (slot_back, first_grad, second_grad)
    slot_back, expert_in_grad, expert_out_grad = lax.map(expert_backward, (dispatch_in, dispatch_grad, expert_in, expert_out))
    normed_two_grad = lax.optimization_barrier(jnp.sum(slot_back[route_flat, slot_index].astype(jnp.float32), axis=1))
    first_logit_grad = (gate_grad[:, 0] - gate_grad[:, 1]) * gate_pair[:, 0] * gate_pair[:, 1]
    logit_grad = (first_logit_grad[:, None] * (route_hot[:, 0, :] - route_hot[:, 1, :])).astype(jnp.bfloat16)
    router_grad = jnp.dot(normed_two.T, logit_grad, preferred_element_type=jnp.float32)
    normed_two_grad = normed_two_grad + jnp.dot(logit_grad, router_weight.T, preferred_element_type=jnp.float32)
    ffn_gain_grad = lax.optimization_barrier(jnp.sum(normed_two_grad * residual_flat * scale_two, axis=0))
    residual_grad = upstream + norm_backward(residual_flat, scale_two, ffn_gain, normed_two_grad)
    residual_grad = residual_grad.reshape(seq_total, seq_length, model_width)

    def attention_backward(running, operands):
        qkv_acc, out_acc, bias_acc, gain_acc = running
        seq_input, attended, log_total, seq_grad = operands
        inputs_wide, scale_one, normed_one, queries, key_rows, value_rows, scores = project_seq(seq_input)
        mixed_grad = seq_grad.astype(jnp.bfloat16)
        out_acc = out_acc + jnp.dot(attended.T, mixed_grad, preferred_element_type=jnp.float32)
        attended_grad = jnp.dot(mixed_grad, attn_out.T, preferred_element_type=jnp.float32).astype(jnp.bfloat16)
        grad_heads = attended_grad.reshape(seq_length, head_count, head_size).astype(jnp.float32)
        probs_full = jnp.exp(scores - log_total)
        probs_low = probs_full.astype(jnp.bfloat16).astype(jnp.float32)
        value_grad = jnp.einsum('hqk,qhe->khe', probs_low, grad_heads)
        prob_grad = jnp.einsum('qhe,khe->hqk', grad_heads, value_rows.astype(jnp.float32))
        row_delta = lax.optimization_barrier(jnp.sum((attended_grad.astype(jnp.float32) * attended.astype(jnp.float32)).reshape(seq_length, head_count, head_size), axis=-1)).T
        score_grad = probs_full * (prob_grad - row_delta[:, :, None])
        bias_acc = bias_acc + jnp.einsum('hqk,qkb->bh', score_grad, bucket_hot, precision=lax.Precision.HIGHEST)
        score_low = score_grad.astype(jnp.bfloat16).astype(jnp.float32)
        query_grad = jnp.einsum('hqk,khe->qhe', score_low, key_rows.astype(jnp.float32)) * score_scale
        key_grad = jnp.einsum('hqk,qhe->khe', score_low, queries.astype(jnp.float32)) * score_scale
        project_grad = jnp.concatenate([query_grad.reshape(seq_length, model_width), key_grad.reshape(seq_length, model_width), value_grad.reshape(seq_length, model_width)], axis=1).astype(jnp.bfloat16)
        qkv_acc = qkv_acc + jnp.dot(normed_one.T, project_grad, preferred_element_type=jnp.float32)
        normed_one_grad = jnp.dot(project_grad, qkv_weight.T, preferred_element_type=jnp.float32)
        gain_acc = gain_acc + lax.optimization_barrier(jnp.sum(normed_one_grad * inputs_wide * scale_one, axis=0))
        input_grad = seq_grad + norm_backward(inputs_wide, scale_one, attn_gain, normed_one_grad)
        return ((qkv_acc, out_acc, bias_acc, gain_acc), input_grad)
    start = (jnp.zeros((model_width, 3 * model_width), jnp.float32), jnp.zeros((model_width, model_width), jnp.float32), jnp.zeros((bucket_count, head_count), jnp.float32), jnp.zeros((model_width,), jnp.float32))
    totals, input_grad = lax.scan(attention_backward, start, (block_input, attended_all, log_totals, residual_grad))
    qkv_grad, attn_out_grad, bias_grad, attn_gain_grad = totals
    return (block_output, input_grad, bias_grad, attn_gain_grad, ffn_gain_grad, qkv_grad, attn_out_grad, router_grad, expert_in_grad, expert_out_grad)
```

```python
import jax
import jax.numpy as jnp
from jax import lax
from jax.sharding import PartitionSpec as P

epsilon = 1e-06
masked_score = -1e30


def rms_scale(values):
    return lax.rsqrt(jnp.mean(values * values, axis=-1, keepdims=True) + epsilon)


def norm_backward(values, inv_rms, gain_vec, upstream):
    weighted = upstream * gain_vec
    inner = jnp.mean(weighted * values, axis=-1, keepdims=True)
    return inv_rms * (weighted - values * inv_rms * inv_rms * inner)


def gelu_grad(pre_gelu, upstream):
    unused_out, pullback = jax.vjp(jax.nn.gelu, pre_gelu)
    return pullback(upstream)[0]


def pad_lanes(values):
    return jnp.pad(values, ((0, 0),) * (values.ndim - 1) + ((0, -values.shape[-1] % 128),))


def three_parts(values):
    high = values.astype(jnp.bfloat16)
    rest = values - high.astype(jnp.float32)
    middle = rest.astype(jnp.bfloat16)
    low = (rest - middle.astype(jnp.float32)).astype(jnp.bfloat16)
    return high, middle, low


def slots_of(routes, expert_count, most_rows):
    block_len = routes.shape[-2]
    hot = (routes[..., None] == jnp.arange(expert_count, dtype=jnp.int32)).astype(jnp.bfloat16)
    either = jnp.sum(hot, axis=-2)
    pos = jnp.arange(block_len, dtype=jnp.int32)
    before = (pos[:, None] > pos[None, :]).astype(jnp.bfloat16)
    earlier = jnp.einsum("ij,...je->...ie", before, either, preferred_element_type=jnp.float32)
    rank = jnp.sum(earlier[..., None, :] * hot, axis=-1).astype(jnp.int32)
    slot = routes * most_rows + rank
    slot_ids = jnp.arange(expert_count * most_rows, dtype=jnp.int32)[:, None]
    first = slot[..., 0][..., None, :] == slot_ids
    second = slot[..., 1][..., None, :] == slot_ids
    return first, second, hot


def on_device(
    block_input,
    cotangent,
    routes,
    buckets,
    position_bias,
    attn_gain,
    ffn_gain,
    qkv_weight,
    attn_out,
    router_weight,
    expert_in,
    expert_out,
):
    seq_count, block_len, model_width = block_input.shape
    bucket_count, head_count = position_bias.shape
    head_size = model_width // head_count
    ep_size = lax.axis_size("ep")
    sq_size = lax.axis_size("sq")
    local_experts = expert_in.shape[0]
    expert_count = local_experts * ep_size
    most_rows = max(2, 3 * block_len // expert_count)
    full_len = block_len * sq_size
    tokens = seq_count * block_len
    score_scale = head_size ** (-0.5)
    pair_count = seq_count * head_count // sq_size
    groups = head_count // pair_count
    pair_width = pair_count * head_size
    f32, bf16 = jnp.float32, jnp.bfloat16

    extra = pad_lanes(
        jnp.concatenate([router_weight, attn_gain[:, None], ffn_gain[:, None]], axis=1)
    )
    packed = lax.all_gather(
        jnp.concatenate([qkv_weight, attn_out, extra], axis=1), ("ep", "sq"), axis=0, tiled=True
    )
    qkv_full = packed[:, : 3 * model_width]
    attn_out_full = packed[:, 3 * model_width : 4 * model_width]
    router_full = packed[:, 4 * model_width : 4 * model_width + expert_count]
    attn_gain_full = packed[:, 4 * model_width + expert_count]
    ffn_gain_full = packed[:, 4 * model_width + expert_count + 1]

    route_rows = -(-seq_count * block_len * 2 // full_len)
    route_flat = jnp.pad(routes.reshape(-1), (0, route_rows * full_len - routes.size))
    lookup = jnp.concatenate([buckets, route_flat.reshape(route_rows, full_len)], axis=0)
    lookup = jnp.pad(lookup, ((0, -lookup.shape[0] % 16), (0, 0))).astype(bf16)
    lookup_all = lax.all_gather(lookup, "sq", axis=0).astype(jnp.int32)
    buckets_all = lookup_all[:, :block_len].reshape(full_len, full_len)
    routes_all = lookup_all[:, block_len : block_len + route_rows].reshape(sq_size, -1)
    routes_all = routes_all[:, : routes.size].reshape(sq_size, seq_count, block_len, 2)

    first, second, hot = slots_of(routes, expert_count, most_rows)
    placing_one, placing_two = first.astype(bf16), second.astype(bf16)
    sent_cot = jnp.einsum("srj,sjd->srd", placing_one + placing_two, cotangent,
                          preferred_element_type=f32).astype(bf16)
    other_hot = (
        jnp.einsum("srj,sje->sre", placing_one, hot[:, :, 1], preferred_element_type=f32)
        + jnp.einsum("srj,sje->sre", placing_two, hot[:, :, 0], preferred_element_type=f32)
    ).astype(bf16)
    sent_cot = jnp.concatenate([sent_cot, pad_lanes(other_hot)], axis=-1)
    sent_width = sent_cot.shape[-1]
    sent_cot = sent_cot.reshape(seq_count, expert_count, most_rows, sent_width)
    sent_cot = jnp.transpose(sent_cot, (1, 0, 2, 3)).reshape(
        ep_size, local_experts, seq_count * most_rows, sent_width
    )
    cot_in = lax.all_to_all(sent_cot, "ep", split_axis=0, concat_axis=0, tiled=True)
    cot_in = lax.all_gather(cot_in, "sq", axis=2, tiled=True)

    inputs_wide = block_input.astype(f32).reshape(tokens, model_width)
    scale_one = rms_scale(inputs_wide)
    normed_one = (inputs_wide * scale_one * attn_gain_full).astype(bf16)
    project = jnp.dot(normed_one, qkv_full, preferred_element_type=f32).astype(bf16)

    project = project.reshape(seq_count, block_len, 3, groups, pair_width)
    project = jnp.transpose(project, (0, 3, 1, 2, 4)).reshape(
        sq_size, block_len, 3 * pair_width
    )
    project = lax.all_to_all(project, "sq", split_axis=0, concat_axis=0, tiled=True)
    project = project.reshape(full_len, 3, pair_count, head_size)
    queries, keys, values = project[:, 0], project[:, 1], project[:, 2]

    bucket_hot = (
        buckets_all[None] == jnp.arange(bucket_count, dtype=jnp.int32)[:, None, None]
    ).astype(bf16)
    my_group = lax.axis_index("sq") % groups
    my_bias = lax.dynamic_slice_in_dim(position_bias, my_group * pair_count, pair_count, axis=1)
    bias_block = jnp.zeros((pair_count, full_len, full_len), f32)
    for bucket in range(bucket_count):
        bias_block = jnp.where(
            (buckets_all == bucket)[None], my_bias[bucket][:, None, None], bias_block
        )
    positions = jnp.arange(full_len, dtype=jnp.int32)
    causal = positions[None, :] <= positions[:, None]
    raw = jnp.einsum("qhe,khe->hqk", queries, keys, preferred_element_type=f32)
    scores = jnp.where(causal, raw * score_scale + bias_block, masked_score)
    row_top = jnp.max(scores, axis=-1, keepdims=True)
    log_total = row_top + jnp.log(jnp.sum(jnp.exp(scores - row_top), axis=-1, keepdims=True))
    probs_full = jnp.exp(scores - log_total)
    probs = probs_full.astype(bf16)
    attended_heads = jnp.einsum(
        "hqk,khe->qhe", probs, values, preferred_element_type=f32
    ).astype(bf16)

    def to_heads(rows):
        rows = rows.reshape(seq_count, block_len, groups, pair_width)
        rows = jnp.transpose(rows, (0, 2, 1, 3)).reshape(sq_size, block_len, pair_width)
        rows = lax.all_to_all(rows, "sq", split_axis=0, concat_axis=0, tiled=True)
        return rows.reshape(full_len, pair_count, head_size)

    def to_tokens(rows, parts):
        rows = rows.reshape(sq_size, block_len, parts * pair_width)
        rows = lax.all_to_all(rows, "sq", split_axis=0, concat_axis=0, tiled=True)
        rows = rows.reshape(seq_count, groups, block_len, parts, pair_width)
        return jnp.transpose(rows, (0, 2, 3, 1, 4)).reshape(tokens, parts * model_width)

    attended = to_tokens(attended_heads, 1)
    residual = inputs_wide + jnp.dot(attended, attn_out_full, preferred_element_type=f32)
    scale_two = rms_scale(residual)
    normed_two = (residual * scale_two * ffn_gain_full).astype(bf16)

    normed_all = lax.all_gather(
        normed_two.reshape(seq_count, block_len, model_width), "sq", axis=0
    )
    first_all, second_all, unused_hot = slots_of(routes_all, expert_count, most_rows)
    placing = (first_all | second_all).astype(bf16)
    outgoing = jnp.einsum(
        "qsrj,qsjd->qsrd", placing, normed_all, preferred_element_type=f32
    ).astype(bf16)
    outgoing = outgoing.reshape(sq_size * seq_count, expert_count, most_rows, model_width)
    row_count = sq_size * seq_count * most_rows
    outgoing = jnp.transpose(outgoing, (1, 0, 2, 3)).reshape(
        ep_size, local_experts, row_count, model_width
    )
    pooled = lax.all_to_all(outgoing, "ep", split_axis=0, concat_axis=0, tiled=True)

    upstream_rows = cot_in[..., :model_width].astype(f32)
    other_rows = cot_in[..., model_width : model_width + expert_count].astype(f32)
    expert_ids = lax.axis_index("ep") * local_experts + jnp.arange(local_experts, dtype=jnp.int32)
    self_hot = (expert_ids[:, None] == jnp.arange(expert_count, dtype=jnp.int32)).astype(f32)
    logits = jnp.einsum("nesd,dx->nesx", pooled, router_full, preferred_element_type=f32)
    apart = other_rows - self_hot[None, :, None, :]
    gate = 1.0 / (1.0 + jnp.exp(jnp.sum(logits * apart, axis=-1, keepdims=True)))
    slot_grad = (gate * upstream_rows).astype(bf16)
    pre_gelu = jnp.einsum("nesd,edf->nesf", pooled, expert_in, preferred_element_type=f32)
    activated = jax.nn.gelu(pre_gelu).astype(bf16)
    value_part = jnp.einsum("nesf,efd->nesd", activated, expert_out, preferred_element_type=f32)
    gate_grad = jnp.sum(value_part * upstream_rows, axis=-1, keepdims=True)
    value_back = lax.all_to_all(
        (gate * value_part).astype(bf16), "ep", split_axis=0, concat_axis=0, tiled=True
    )
    act_grad = jnp.einsum("nesd,efd->nesf", slot_grad, expert_out, preferred_element_type=f32)
    pre_grad = gelu_grad(pre_gelu, act_grad).astype(bf16)
    filled = jnp.sum(other_rows, axis=-1, keepdims=True)
    logit_rows = (-gate_grad * gate * (1.0 - gate) * filled * apart).astype(bf16)
    back_part = jnp.einsum("nesf,edf->nesd", pre_grad, expert_in, preferred_element_type=f32)
    back_part = back_part + jnp.einsum(
        "nesx,dx->nesd", logit_rows, router_full, preferred_element_type=f32
    )
    slots_back = lax.all_to_all(
        back_part.astype(bf16), "ep", split_axis=0, concat_axis=0, tiled=True
    )
    expert_out_grad = jnp.einsum("nesf,nesd->efd", activated, slot_grad, preferred_element_type=f32)
    expert_in_grad = jnp.einsum("nesd,nesf->edf", pooled, pre_grad, preferred_element_type=f32)
    router_part = jnp.einsum("nesd,nesx->dx", pooled, logit_rows, preferred_element_type=f32)

    def to_sequences(rows):
        rows = rows.reshape(expert_count, sq_size, seq_count, most_rows, model_width)
        rows = jnp.transpose(rows, (1, 2, 0, 3, 4)).reshape(
            sq_size, seq_count, expert_count * most_rows, model_width
        )
        mixed = jnp.einsum(
            "qsrj,qsrd->qsjd", placing, rows, preferred_element_type=f32
        ).astype(bf16)
        mixed = lax.psum_scatter(mixed, "sq", scatter_dimension=0, tiled=False)
        return mixed.reshape(tokens, model_width).astype(f32)

    expert_mix = to_sequences(value_back)
    normed_two_grad = to_sequences(slots_back)
    block_output = (residual + expert_mix).astype(bf16)
    upstream = cotangent.reshape(tokens, model_width).astype(f32)
    ffn_gain_part = jnp.sum(normed_two_grad * residual * scale_two, axis=0)
    residual_grad = upstream + norm_backward(residual, scale_two, ffn_gain_full, normed_two_grad)
    mixed_grad = residual_grad.astype(bf16)
    attended_grad = jnp.dot(mixed_grad, attn_out_full.T, preferred_element_type=f32).astype(bf16)
    grad_heads = to_heads(attended_grad)
    attn_out_part = jnp.dot(attended.T, mixed_grad, preferred_element_type=f32)
    device_count = ep_size * sq_size

    def scatter_rows(parts):
        columns = jnp.concatenate(
            parts[:1] + [pad_lanes(jnp.concatenate(parts[1:], axis=1))], axis=1
        ).astype(bf16)
        columns = columns.reshape(device_count, -1, columns.shape[1])
        return lax.psum_scatter(
            columns, ("ep", "sq"), scatter_dimension=0, tiled=False
        ).astype(f32)

    out_sums = scatter_rows([attn_out_part, router_part, ffn_gain_part[:, None]])
    attn_out_grad = out_sums[:, :model_width]
    router_grad = out_sums[:, model_width : model_width + expert_count]
    ffn_gain_grad = out_sums[:, model_width + expert_count]

    value_grad = jnp.einsum("hqk,qhe->khe", probs, grad_heads, preferred_element_type=f32)
    prob_grad = jnp.einsum("qhe,khe->hqk", grad_heads, values, preferred_element_type=f32)
    row_delta = jnp.sum(grad_heads.astype(f32) * attended_heads.astype(f32), axis=-1)
    score_grad = probs_full * (prob_grad - row_delta.T[:, :, None])
    score_low = score_grad.astype(bf16)
    query_grad = jnp.einsum("hqk,khe->qhe", score_low, keys, preferred_element_type=f32)
    key_grad = jnp.einsum("hqk,qhe->khe", score_low, queries, preferred_element_type=f32)
    project_grad = jnp.stack(
        [query_grad * score_scale, key_grad * score_scale, value_grad], axis=1
    ).astype(bf16)
    project_grad = to_tokens(project_grad, 3)
    score_rest = (score_grad - score_low.astype(f32)).astype(bf16)
    bias_part = jnp.einsum(
        "hqk,bqk->bh", score_low, bucket_hot, preferred_element_type=f32
    ) + jnp.einsum("hqk,bqk->bh", score_rest, bucket_hot, preferred_element_type=f32)
    bias_wide = lax.dynamic_update_slice_in_dim(
        jnp.zeros((bucket_count, head_count), f32), bias_part, my_group * pair_count, axis=1
    )
    bias_all = lax.all_gather(pad_lanes(bias_wide), ("ep", "sq"), axis=0)
    bias_grad = jnp.sum(bias_all, axis=0)[:, :head_count]

    qkv_part = jnp.dot(normed_one.T, project_grad, preferred_element_type=f32)
    normed_one_grad = jnp.dot(project_grad, qkv_full.T, preferred_element_type=f32)
    attn_gain_part = jnp.sum(normed_one_grad * inputs_wide * scale_one, axis=0)
    input_grad = residual_grad + norm_backward(
        inputs_wide, scale_one, attn_gain_full, normed_one_grad
    )
    qkv_sums = scatter_rows([qkv_part, attn_gain_part[:, None]])
    return (
        block_output.reshape(seq_count, block_len, model_width),
        input_grad.reshape(seq_count, block_len, model_width),
        bias_grad,
        qkv_sums[:, 3 * model_width],
        ffn_gain_grad,
        qkv_sums[:, : 3 * model_width],
        attn_out_grad,
        router_grad,
        expert_in_grad,
        expert_out_grad,
    )


def solution(mesh):
    in_specs = (
        P("ep", "sq", None),
        P("ep", "sq", None),
        P("ep", "sq", None),
        P("sq", None),
        P(),
        P(("ep", "sq")),
        P(("ep", "sq")),
        P(("ep", "sq"), None),
        P(("ep", "sq"), None),
        P(("ep", "sq"), None),
        P("ep", None, "sq"),
        P("ep", "sq", None),
    )
    out_specs = (
        P("ep", "sq", None),
        P("ep", "sq", None),
        P(),
        P(("ep", "sq")),
        P(("ep", "sq")),
        P(("ep", "sq"), None),
        P(("ep", "sq"), None),
        P(("ep", "sq"), None),
        P("ep", None, "sq"),
        P("ep", "sq", None),
    )
    return jax.shard_map(
        on_device, mesh=mesh, in_specs=in_specs, out_specs=out_specs, check_vma=False
    )
```

```python
import jax
import jax.numpy as jnp
from jax import lax
from jax.sharding import PartitionSpec as P

epsilon = 1e-06
masked_score = -1e30


def rms_scale(values):
    return lax.rsqrt(jnp.mean(values * values, axis=-1, keepdims=True) + epsilon)


def norm_backward(values, inv_rms, gain_vec, upstream):
    weighted = upstream * gain_vec
    inner = jnp.mean(weighted * values, axis=-1, keepdims=True)
    return inv_rms * (weighted - values * inv_rms * inv_rms * inner)


def gelu_grad(pre_gelu, upstream):
    unused_out, pullback = jax.vjp(jax.nn.gelu, pre_gelu)
    return pullback(upstream)[0]


def pad_lanes(values):
    return jnp.pad(values, ((0, 0),) * (values.ndim - 1) + ((0, -values.shape[-1] % 128),))


def three_parts(values):
    high = values.astype(jnp.bfloat16)
    rest = values - high.astype(jnp.float32)
    middle = rest.astype(jnp.bfloat16)
    low = (rest - middle.astype(jnp.float32)).astype(jnp.bfloat16)
    return high, middle, low


def slots_of(routes, expert_count, most_rows):
    block_len = routes.shape[-2]
    hot = (routes[..., None] == jnp.arange(expert_count, dtype=jnp.int32)).astype(jnp.bfloat16)
    either = jnp.sum(hot, axis=-2)
    pos = jnp.arange(block_len, dtype=jnp.int32)
    before = (pos[:, None] > pos[None, :]).astype(jnp.bfloat16)
    earlier = jnp.einsum("ij,...je->...ie", before, either, preferred_element_type=jnp.float32)
    rank = jnp.sum(earlier[..., None, :] * hot, axis=-1).astype(jnp.int32)
    slot = routes * most_rows + rank
    slot_ids = jnp.arange(expert_count * most_rows, dtype=jnp.int32)[:, None]
    first = slot[..., 0][..., None, :] == slot_ids
    second = slot[..., 1][..., None, :] == slot_ids
    return first, second, hot


def on_device(
    block_input,
    cotangent,
    routes,
    buckets,
    position_bias,
    attn_gain,
    ffn_gain,
    qkv_weight,
    attn_out,
    router_weight,
    expert_in,
    expert_out,
):
    seq_count, block_len, model_width = block_input.shape
    bucket_count, head_count = position_bias.shape
    head_size = model_width // head_count
    ep_size = lax.axis_size("ep")
    sq_size = lax.axis_size("sq")
    local_experts = expert_in.shape[0]
    expert_count = local_experts * ep_size
    most_rows = max(2, 3 * block_len // expert_count)
    full_len = block_len * sq_size
    tokens = seq_count * block_len
    score_scale = head_size ** (-0.5)
    pair_count = seq_count * head_count // sq_size
    groups = head_count // pair_count
    pair_width = pair_count * head_size
    f32, bf16 = jnp.float32, jnp.bfloat16

    extra = pad_lanes(
        jnp.concatenate([router_weight, attn_gain[:, None], ffn_gain[:, None]], axis=1)
    )
    packed = lax.all_gather(
        jnp.concatenate([qkv_weight, attn_out, extra], axis=1), ("ep", "sq"), axis=0, tiled=True
    )
    qkv_full = packed[:, : 3 * model_width]
    attn_out_full = packed[:, 3 * model_width : 4 * model_width]
    router_full = packed[:, 4 * model_width : 4 * model_width + expert_count]
    attn_gain_full = packed[:, 4 * model_width + expert_count]
    ffn_gain_full = packed[:, 4 * model_width + expert_count + 1]

    route_rows = -(-seq_count * block_len * 2 // full_len)
    route_flat = jnp.pad(routes.reshape(-1), (0, route_rows * full_len - routes.size))
    lookup = jnp.concatenate([buckets, route_flat.reshape(route_rows, full_len)], axis=0)
    lookup = jnp.pad(lookup, ((0, -lookup.shape[0] % 16), (0, 0))).astype(bf16)
    lookup_all = lax.all_gather(lookup, "sq", axis=0).astype(jnp.int32)
    buckets_all = lookup_all[:, :block_len].reshape(full_len, full_len)
    routes_all = lookup_all[:, block_len : block_len + route_rows].reshape(sq_size, -1)
    routes_all = routes_all[:, : routes.size].reshape(sq_size, seq_count, block_len, 2)

    cot_all = lax.all_gather(cotangent, "sq", axis=0)
    first, second, hot = slots_of(routes_all, expert_count, most_rows)
    placing_one, placing_two = first.astype(bf16), second.astype(bf16)
    placing = placing_one + placing_two
    row_count = sq_size * seq_count * most_rows

    def to_experts(rows):
        rows = rows.reshape(sq_size * seq_count, expert_count, most_rows, rows.shape[-1])
        rows = jnp.transpose(rows, (1, 0, 2, 3)).reshape(
            ep_size, local_experts, row_count, rows.shape[-1]
        )
        return [
            lax.all_to_all(rows[:, own], "ep", split_axis=0, concat_axis=0, tiled=True)
            for own in range(local_experts)
        ]

    sent_cot = jnp.einsum(
        "qsrj,qsjd->qsrd", placing, cot_all, preferred_element_type=f32
    ).astype(bf16)
    other_hot = (
        jnp.einsum("qsrj,qsje->qsre", placing_one, hot[..., 1, :], preferred_element_type=f32)
        + jnp.einsum("qsrj,qsje->qsre", placing_two, hot[..., 0, :], preferred_element_type=f32)
    ).astype(bf16)
    cot_in = to_experts(jnp.concatenate([sent_cot, pad_lanes(other_hot)], axis=-1))

    inputs_wide = block_input.astype(f32).reshape(tokens, model_width)
    scale_one = rms_scale(inputs_wide)
    normed_one = (inputs_wide * scale_one * attn_gain_full).astype(bf16)
    project = jnp.dot(normed_one, qkv_full, preferred_element_type=f32).astype(bf16)

    project = project.reshape(seq_count, block_len, 3, groups, pair_width)
    project = jnp.transpose(project, (0, 3, 1, 2, 4)).reshape(
        sq_size, block_len, 3 * pair_width
    )
    project = lax.all_to_all(project, "sq", split_axis=0, concat_axis=0, tiled=True)
    project = project.reshape(full_len, 3, pair_count, head_size)
    queries, keys, values = project[:, 0], project[:, 1], project[:, 2]

    bucket_hot = (
        buckets_all[None] == jnp.arange(bucket_count, dtype=jnp.int32)[:, None, None]
    ).astype(bf16)
    my_group = lax.axis_index("sq") % groups
    my_bias = lax.dynamic_slice_in_dim(position_bias, my_group * pair_count, pair_count, axis=1)
    bias_block = jnp.zeros((pair_count, full_len, full_len), f32)
    for bucket in range(bucket_count):
        bias_block = jnp.where(
            (buckets_all == bucket)[None], my_bias[bucket][:, None, None], bias_block
        )
    positions = jnp.arange(full_len, dtype=jnp.int32)
    causal = positions[None, :] <= positions[:, None]
    raw = jnp.einsum("qhe,khe->hqk", queries, keys, preferred_element_type=f32)
    scores = jnp.where(causal, raw * score_scale + bias_block, masked_score)
    row_top = jnp.max(scores, axis=-1, keepdims=True)
    log_total = row_top + jnp.log(jnp.sum(jnp.exp(scores - row_top), axis=-1, keepdims=True))
    probs_full = jnp.exp(scores - log_total)
    probs = probs_full.astype(bf16)
    attended_heads = jnp.einsum(
        "hqk,khe->qhe", probs, values, preferred_element_type=f32
    ).astype(bf16)

    def to_heads(rows):
        rows = rows.reshape(seq_count, block_len, groups, pair_width)
        rows = jnp.transpose(rows, (0, 2, 1, 3)).reshape(sq_size, block_len, pair_width)
        rows = lax.all_to_all(rows, "sq", split_axis=0, concat_axis=0, tiled=True)
        return rows.reshape(full_len, pair_count, head_size)

    def to_tokens(rows, parts):
        rows = rows.reshape(sq_size, block_len, parts * pair_width)
        rows = lax.all_to_all(rows, "sq", split_axis=0, concat_axis=0, tiled=True)
        rows = rows.reshape(seq_count, groups, block_len, parts, pair_width)
        return jnp.transpose(rows, (0, 2, 3, 1, 4)).reshape(tokens, parts * model_width)

    attended_heads, cot_in = lax.optimization_barrier((attended_heads, cot_in))
    attended = to_tokens(attended_heads, 1)
    residual = inputs_wide + jnp.dot(attended, attn_out_full, preferred_element_type=f32)
    scale_two = rms_scale(residual)
    normed_two = (residual * scale_two * ffn_gain_full).astype(bf16)

    normed_all = lax.all_to_all(
        jnp.broadcast_to(
            normed_two.reshape(1, seq_count, block_len, model_width),
            (sq_size, seq_count, block_len, model_width),
        ),
        "sq", split_axis=0, concat_axis=0, tiled=True,
    )
    outgoing = jnp.einsum(
        "qsrj,qsjd->qsrd", placing, normed_all, preferred_element_type=f32
    ).astype(bf16)
    pooled_in = to_experts(outgoing)

    values_back, slots_back, out_grads, in_grads = [], [], [], []
    router_part = jnp.zeros((model_width, expert_count), f32)
    for own in range(local_experts):
        pooled, weight_in, weight_out = pooled_in[own], expert_in[own], expert_out[own]
        upstream_rows = cot_in[own][..., :model_width].astype(f32)
        other_rows = cot_in[own][..., model_width : model_width + expert_count].astype(f32)
        expert_id = lax.axis_index("ep") * local_experts + own
        self_hot = (expert_id == jnp.arange(expert_count, dtype=jnp.int32)).astype(f32)
        logits = jnp.einsum("nsd,dx->nsx", pooled, router_full, preferred_element_type=f32)
        apart = other_rows - self_hot
        gate = 1.0 / (1.0 + jnp.exp(jnp.sum(logits * apart, axis=-1, keepdims=True)))
        slot_grad = (gate * upstream_rows).astype(bf16)
        pre_gelu = jnp.einsum("nsd,df->nsf", pooled, weight_in, preferred_element_type=f32)
        activated = jax.nn.gelu(pre_gelu).astype(bf16)
        value_part = jnp.einsum("nsf,fd->nsd", activated, weight_out, preferred_element_type=f32)
        gate_grad = jnp.sum(value_part * upstream_rows, axis=-1, keepdims=True)
        value_send = (gate * value_part).astype(bf16)
        value_send, slot_grad = lax.optimization_barrier((value_send, slot_grad))
        values_back.append(
            lax.all_to_all(value_send, "ep", split_axis=0, concat_axis=0, tiled=True)
        )
        act_grad = jnp.einsum("nsd,fd->nsf", slot_grad, weight_out, preferred_element_type=f32)
        pre_grad = gelu_grad(pre_gelu, act_grad).astype(bf16)
        filled = jnp.sum(other_rows, axis=-1, keepdims=True)
        logit_rows = (-gate_grad * gate * (1.0 - gate) * filled * apart).astype(bf16)
        back_part = jnp.einsum("nsf,df->nsd", pre_grad, weight_in, preferred_element_type=f32)
        back_part = back_part + jnp.einsum(
            "nsx,dx->nsd", logit_rows, router_full, preferred_element_type=f32
        )
        slots_back.append(
            lax.all_to_all(back_part.astype(bf16), "ep", split_axis=0, concat_axis=0, tiled=True)
        )
        out_grads.append(
            jnp.einsum("nsf,nsd->fd", activated, slot_grad, preferred_element_type=f32)
        )
        in_grads.append(jnp.einsum("nsd,nsf->df", pooled, pre_grad, preferred_element_type=f32))
        router_part = router_part + jnp.einsum(
            "nsd,nsx->dx", pooled, logit_rows, preferred_element_type=f32
        )
    expert_out_grad, expert_in_grad = jnp.stack(out_grads), jnp.stack(in_grads)

    def summed(blocks, axis):
        arrived = lax.all_to_all(blocks, axis, split_axis=0, concat_axis=0, tiled=True)
        return jnp.sum(arrived.astype(f32), axis=0)

    def to_sequences(rows):
        rows = jnp.stack(rows, axis=1)
        rows = rows.reshape(expert_count, sq_size, seq_count, most_rows, model_width)
        rows = jnp.transpose(rows, (1, 2, 0, 3, 4)).reshape(
            sq_size, seq_count, expert_count * most_rows, model_width
        )
        mixed = jnp.einsum(
            "qsrj,qsrd->qsjd", placing, rows, preferred_element_type=f32
        ).astype(bf16)
        return summed(mixed, "sq").reshape(tokens, model_width)

    expert_mix = to_sequences(values_back)
    normed_two_grad = to_sequences(slots_back)
    block_output = (residual + expert_mix).astype(bf16)
    upstream = cotangent.reshape(tokens, model_width).astype(f32)
    ffn_gain_part = jnp.sum(normed_two_grad * residual * scale_two, axis=0)
    residual_grad = upstream + norm_backward(residual, scale_two, ffn_gain_full, normed_two_grad)
    mixed_grad = residual_grad.astype(bf16)
    attended_grad = jnp.dot(mixed_grad, attn_out_full.T, preferred_element_type=f32).astype(bf16)
    grad_heads = to_heads(attended_grad)
    attn_out_part = jnp.dot(attended.T, mixed_grad, preferred_element_type=f32)
    device_count = ep_size * sq_size

    def packed_rows(parts):
        columns = jnp.concatenate(
            parts[:1] + [pad_lanes(jnp.concatenate(parts[1:], axis=1))], axis=1
        )
        return columns.astype(bf16).reshape(device_count, -1, columns.shape[1])

    def exchange_first(parts):
        blocks = packed_rows(parts)
        blocks = blocks.reshape(ep_size, sq_size, blocks.shape[1], blocks.shape[2])
        return summed(blocks, "ep").astype(bf16)

    out_blocks = exchange_first([attn_out_part, router_part, ffn_gain_part[:, None]])

    value_grad = jnp.einsum("hqk,qhe->khe", probs, grad_heads, preferred_element_type=f32)
    prob_grad = jnp.einsum("qhe,khe->hqk", grad_heads, values, preferred_element_type=f32)
    row_delta = jnp.sum(grad_heads.astype(f32) * attended_heads.astype(f32), axis=-1)
    score_grad = probs_full * (prob_grad - row_delta.T[:, :, None])
    score_low = score_grad.astype(bf16)
    query_grad = jnp.einsum("hqk,khe->qhe", score_low, keys, preferred_element_type=f32)
    key_grad = jnp.einsum("hqk,qhe->khe", score_low, queries, preferred_element_type=f32)
    project_grad = jnp.stack(
        [query_grad * score_scale, key_grad * score_scale, value_grad], axis=1
    ).astype(bf16)
    project_grad, out_blocks = lax.optimization_barrier((project_grad, out_blocks))
    out_sums = summed(out_blocks, "sq")
    attn_out_grad = out_sums[:, :model_width]
    router_grad = out_sums[:, model_width : model_width + expert_count]
    ffn_gain_grad = out_sums[:, model_width + expert_count]
    project_grad = to_tokens(project_grad, 3)
    score_rest = (score_grad - score_low.astype(f32)).astype(bf16)
    bias_part = jnp.einsum(
        "hqk,bqk->bh", score_low, bucket_hot, preferred_element_type=f32
    ) + jnp.einsum("hqk,bqk->bh", score_rest, bucket_hot, preferred_element_type=f32)
    bias_wide = lax.dynamic_update_slice_in_dim(
        jnp.zeros((bucket_count, head_count), f32), bias_part, my_group * pair_count, axis=1
    )
    bias_wide = jnp.broadcast_to(
        pad_lanes(bias_wide.reshape(1, -1))[None], (device_count, 1, bias_wide.size + -bias_wide.size % 128)
    )
    bias_grad = summed(bias_wide, ("ep", "sq")).reshape(-1)[: bucket_count * head_count]
    bias_grad = bias_grad.reshape(bucket_count, head_count)

    qkv_part = jnp.dot(normed_one.T, project_grad, preferred_element_type=f32)
    normed_one_grad = jnp.dot(project_grad, qkv_full.T, preferred_element_type=f32)
    attn_gain_part = jnp.sum(normed_one_grad * inputs_wide * scale_one, axis=0)
    input_grad = residual_grad + norm_backward(
        inputs_wide, scale_one, attn_gain_full, normed_one_grad
    )
    qkv_sums = summed(exchange_first([qkv_part, attn_gain_part[:, None]]), "sq")
    return (
        block_output.reshape(seq_count, block_len, model_width),
        input_grad.reshape(seq_count, block_len, model_width),
        bias_grad,
        qkv_sums[:, 3 * model_width],
        ffn_gain_grad,
        qkv_sums[:, : 3 * model_width],
        attn_out_grad,
        router_grad,
        expert_in_grad,
        expert_out_grad,
    )


def solution(mesh):
    in_specs = (
        P("ep", "sq", None),
        P("ep", "sq", None),
        P("ep", "sq", None),
        P("sq", None),
        P(),
        P(("ep", "sq")),
        P(("ep", "sq")),
        P(("ep", "sq"), None),
        P(("ep", "sq"), None),
        P(("ep", "sq"), None),
        P("ep", None, "sq"),
        P("ep", "sq", None),
    )
    out_specs = (
        P("ep", "sq", None),
        P("ep", "sq", None),
        P(),
        P(("ep", "sq")),
        P(("ep", "sq")),
        P(("ep", "sq"), None),
        P(("ep", "sq"), None),
        P(("ep", "sq"), None),
        P("ep", None, "sq"),
        P("ep", "sq", None),
    )
    return jax.shard_map(
        on_device, mesh=mesh, in_specs=in_specs, out_specs=out_specs, check_vma=False
    )
```
